32 devices in a mesh: layer: 2 (over x), row: 16 (over z, y, core).
Axes of the slice: x: 2, y: 2, z: 4, core: 2. Of those that a mesh axis runs over, the one named last changes fastest.
Arguments:
- leaf_rhs: float32 [2, 16, 256, 384], P('layer', 'row'), may hold values from -6 to 6
- leaf_inverse: float32 [2, 16, 256, 256], P('layer', 'row'), may hold values from -0.375 to 0.375
- leaf_coupling: float32 [2, 16, 4, 512, 256], P('layer', 'row'), may hold values from -0.09375 to 0.09375
- parent: int32 [2, 16], P('layer', 'row'), may hold values from 0 to 3
- sep_rhs: float32 [2, 4, 512, 384], P('layer', None, 'row'), may hold values from -6 to 6
- sep_inverse: float32 [2, 4, 512, 512], P('layer', None, 'row'), may hold values from -0.25 to 0.25
- sep_coupling: float32 [2, 3, 512, 512], P('layer', None, 'row'), may hold values from -0.125 to 0.125
- root_coupling: float32 [2, 512, 512], P('layer', 'row'), may hold values from -0.1875 to 0.1875
- root_rhs: float32 [512, 384], P('row'), may hold values from -6 to 6
- root_inverse: float32 [512, 512], P('row'), may hold values from -0.25 to 0.25
Outputs:
- sep_solution: float32 [2, 4, 512, 384], P('layer', None, 'row')
- root_solution: float32 [512, 384], P('row')
The draws below stay inside these ranges and needn't reach their ends.
All inputs are finite; a program needn't handle non-finite values.
Results may differ from the reference program's by a relative error of at most 0.0003.
Values sent between devices are 32-bit elements; how exact they have to be, the bound alone decides.
A program may use at most 64 MiB of HBM per device.

```python
import jax
import jax.numpy as jnp
from jax import lax

W = 512
SEPS = 4
LEAF = 256
R = 384
N_LAYER = 2
N_ROW = 16


def with_ends(array, own_key, low, largest):
    index_at = [jax.random.randint(jax.random.fold_in(own_key, axis), (), 0, length) for axis, length in enumerate(array.shape)]
    widest = array.shape.index(max(array.shape))
    beside = index_at[:widest] + [(index_at[widest] + 1) % array.shape[widest]] + index_at[widest + 1:]
    return array.at[tuple(index_at)].set(low).at[tuple(beside)].set(largest)


def block_levels(rng, dims, shards, low, largest):
    def one(position, shards_of):
        steps = jax.random.uniform(jax.random.fold_in(jax.random.fold_in(rng, 6), position), (shards_of,), jnp.float32, low / len(shards), largest / len(shards))
        return jnp.repeat(jnp.exp(steps), dims[position] // shards_of).reshape((-1,) + (1,) * (len(dims) - position - 1))

    factor_of = one(*shards[0])
    for cut in shards[1:]:
        factor_of = factor_of * one(*cut)
    return factor_of


def normal_values(own_key, shape, scale, bound, cuts=(), kind=jnp.bfloat16):
    factor_of = block_levels(own_key, shape, cuts, -0.22, 0.18) if cuts else 1.0
    values = jax.random.normal(own_key, shape, jnp.float32) * scale * factor_of
    return jnp.minimum(jnp.maximum(values, -bound), bound).astype(kind)


def setup_inputs(seed: int = 0) -> dict:
    seeds = jax.random.split(jax.random.key(seed), 11)
    return {
        "leaf_rhs": normal_values(seeds[0], (N_LAYER, N_ROW, LEAF, R), 1.0, 6.0, ((0, 2), (1, 16)), jnp.float32),
        "leaf_inverse": normal_values(seeds[1], (N_LAYER, N_ROW, LEAF, LEAF), LEAF ** -0.5, 0.375, ((0, 2), (1, 16)), jnp.float32),
        "leaf_coupling": normal_values(seeds[2], (N_LAYER, N_ROW, SEPS, W, LEAF), (LEAF * N_ROW) ** -0.5, 0.09375, ((0, 2), (1, 16)), jnp.float32),
        "parent": with_ends(jax.random.randint(seeds[3], (N_LAYER, N_ROW), 0, SEPS), jax.random.fold_in(seeds[3], 1), 0, SEPS - 1).astype(jnp.int32),
        "sep_rhs": normal_values(seeds[4], (N_LAYER, SEPS, W, R), 1.0, 6.0, ((0, 2), (2, 16)), jnp.float32),
        "sep_inverse": normal_values(seeds[5], (N_LAYER, SEPS, W, W), W ** -0.5, 0.25, ((0, 2), (2, 16)), jnp.float32),
        "sep_coupling": normal_values(seeds[6], (N_LAYER, SEPS - 1, W, W), (4 * W) ** -0.5, 0.125, ((0, 2), (2, 16)), jnp.float32),
        "root_coupling": normal_values(seeds[7], (N_LAYER, W, W), (W * N_LAYER) ** -0.5, 0.1875, ((0, 2), (1, 16)), jnp.float32),
        "root_rhs": normal_values(seeds[8], (W, R), 1.0, 6.0, ((0, 16),), jnp.float32),
        "root_inverse": normal_values(seeds[9], (W, W), W ** -0.5, 0.25, ((0, 16),), jnp.float32),
    }


def reference(leaf_rhs, leaf_inverse, leaf_coupling, parent, sep_rhs, sep_inverse, sep_coupling, root_coupling, root_rhs, root_inverse):
    highest = lax.Precision.HIGHEST

    def one_layer(inputs):
        rhs_layer, inverse_layer, coupling_layer, parent_layer, sep_rhs_layer, sep_inverse_layer, chain_layer = inputs
        leaf_solution = jnp.einsum('rab,rbc->rac', inverse_layer, rhs_layer, precision=highest)
        levels = jnp.arange(SEPS, dtype=jnp.int32)
        keep_mask = (levels[None, :] >= parent_layer[:, None]).astype(jnp.float32)
        coupled = jnp.einsum('rkwb,rbc,rk->kwc', coupling_layer, leaf_solution, keep_mask, precision=highest)
        residual = sep_rhs_layer - coupled
        solved = []
        previous = None
        for k in range(SEPS):
            current = jnp.dot(sep_inverse_layer[k], residual[k], precision=highest)
            if k > 0:
                current = current - jnp.dot(chain_layer[k - 1], previous, precision=highest)
            solved.append(current)
            previous = current
        return jnp.stack(solved)

    sep_solution = lax.map(one_layer, (leaf_rhs, leaf_inverse, leaf_coupling, parent, sep_rhs, sep_inverse, sep_coupling))
    root_update = jnp.einsum('lwv,lvc->wc', root_coupling, sep_solution[:, SEPS - 1], precision=highest)
    root_residual = root_rhs - root_update
    root_solution = jnp.dot(root_inverse, root_residual, precision=highest)
    return sep_solution, root_solution
```

```python
import functools

import jax
import jax.numpy as jnp
from jax import lax
from jax.experimental import pallas as pl
from jax.experimental.pallas import tpu as pltpu
from jax.sharding import PartitionSpec as P

MESH = pl.DeviceIdType.MESH
NN = (((1,), (0,)), ((), ()))
NT = (((1,), (1,)), ((), ()))
HALVES = 2
LAG = 1


def split(a):
    high = a.astype(jnp.bfloat16)
    return high, (a - high.astype(jnp.float32)).astype(jnp.bfloat16)


def dot3(a, b, dims):
    (ah, al), (bh, bl) = a, b
    dot = functools.partial(lax.dot_general, dimension_numbers=dims, preferred_element_type=jnp.float32)
    return dot(ah, bh) + (dot(ah, bl) + dot(al, bh))


def kernel(
    n_z,
    parent,
    leaf_rhs,
    leaf_inverse,
    leaf_coupling,
    sep_rhs,
    sep_inverse,
    sep_coupling,
    root_coupling,
    root_rhs,
    root_inverse,
    sep_out,
    root_out,
    g_inv,
    g_chain,
    g_rc,
    g_rr,
    g_ri,
    part,
    from_core,
    to_y,
    from_y,
    mine,
    fwd,
    bwd,
    from_left,
    from_right,
    total,
    solved,
    padded,
    turned,
    pieces,
    root_send,
    root_recv,
    root_full,
    w_send,
    w_recv,
    c_send,
    c_recv,
    y_send,
    y_recv,
    f_send,
    f_recv,
    b_send,
    b_recv,
    a_send,
    a_recv,
    o_send,
    o_recv,
    x_send,
    x_recv,
):
    seps, rows, right = sep_rhs.shape
    width = sep_inverse.shape[2]
    zrows = width // n_z
    half, quarter = right // 2, right // 4
    sub = quarter // HALVES

    layer = lax.axis_index("layer")
    me = lax.axis_index("row")
    z, y, c = me // 4, (me // 2) % 2, me % 2
    plane = 2 * y + c
    base = 4 * z

    def at(zz, yy, cc):
        return (layer, 4 * zz + 2 * yy + cc)

    core_peer = at(z, y, 1 - c)
    y_peer = at(z, 1 - y, c)
    far_peer = at(z, 1 - y, 1 - c)
    x_peer = (1 - layer, me)
    left, right_peer = (layer, me - 4), (layer, me + 4)
    z_peers = [at((z + d) % n_z, y, c) for d in range(1, n_z)]
    plane_peers = [core_peer, y_peer, far_peer]

    def remote(src, dst, send, recv, peer):
        return pltpu.make_async_remote_copy(
            src_ref=src, dst_ref=dst, send_sem=send, recv_sem=recv, device_id=peer, device_id_type=MESH
        )

    barrier = pltpu.get_barrier_semaphore()
    peers = plane_peers + z_peers + [x_peer]
    for peer in peers:
        pl.semaphore_signal(barrier, inc=1, device_id=peer, device_id_type=MESH)
    pl.semaphore_wait(barrier, len(peers))

    own_rows = pl.ds(pl.multiple_of(plane * rows, rows), rows)
    y_rows = pl.ds(pl.multiple_of((2 * (1 - y) + c) * rows, rows), rows)
    weights = [
        (sep_inverse, g_inv, True),
        (sep_coupling, g_chain, True),
        (root_coupling, g_rc, False),
        (root_rhs, g_rr, False),
        (root_inverse, g_ri, False),
    ]

    def slot(ref, deep, where):
        return ref.at[:, where, :] if deep else ref.at[where, :]

    def weight(way, n):
        source, dest, deep = weights[n]
        if way == 2:
            source, where = slot(dest, deep, y_rows), y_rows
        else:
            where = own_rows
        return remote(
            source,
            slot(dest, deep, where),
            w_send.at[way, n],
            w_recv.at[way, n],
            y_peer if way == 0 else core_peer,
        )

    def weight_start(way, which):
        for n in which:
            weight(way, n).start()

    weight_start(0, (0,))
    g_inv[:, own_rows, :] = sep_inverse[...]
    g_chain[:, own_rows, :] = sep_coupling[...]
    g_rc[own_rows, :] = root_coupling[...]
    g_rr[own_rows, :] = root_rhs[...]
    g_ri[own_rows, :] = root_inverse[...]

    leaf = dot3(split(leaf_inverse[...]), split(leaf_rhs[...]), NN)
    leaf_t = split(leaf.T)
    zlanes = pl.ds(pl.multiple_of(z * zrows, 128), zrows)
    core_cols = pl.ds(pl.multiple_of(half * c, 8), half)
    other_core_cols = pl.ds(pl.multiple_of(half * (1 - c), 8), half)
    padded[...] = jnp.zeros_like(padded)

    def core_copy(k):
        return remote(
            part.at[k, other_core_cols, :], from_core.at[k], c_send.at[k], c_recv.at[k], core_peer
        )

    def stage_a(k):
        keep = jnp.where(parent[0, 0] <= k, -1.0, 0.0).astype(jnp.float32)
        part[k] = dot3(leaf_t, split(leaf_coupling[k]), NT) * keep
        padded[own_rows, :] = sep_rhs[k]
        part[k, :, zlanes] += padded[...].T
        core_copy(k).start()

    own_y = pl.multiple_of(quarter * y, 8)
    peer_y = pl.multiple_of(quarter * (1 - y), 8)

    def y_copy(k, h):
        where = pl.ds(h * sub, sub)
        return remote(
            to_y.at[k, where, :], from_y.at[k, where, :], y_send.at[k, h], y_recv.at[k, h], y_peer
        )

    def stage_b(k):
        core_copy(k).wait_recv()
        to_y[k] = (
            part[k, pl.ds(pl.multiple_of(half * c + peer_y, 8), quarter), :]
            + from_core[k, pl.ds(peer_y, quarter), :]
        )
        for h in range(HALVES):
            y_copy(k, h).start()

    def fwd_copy(k, h):
        where = pl.ds(h * sub, sub)
        return remote(
            fwd.at[k, where, :], from_left.at[k, where, :], f_send.at[k, h], f_recv.at[k, h], right_peer
        )

    def bwd_copy(k, h):
        where = pl.ds(h * sub, sub)
        return remote(
            bwd.at[k, where, :], from_right.at[k, where, :], b_send.at[k, h], b_recv.at[k, h], left
        )

    def stage_c(k, h):
        where = pl.ds(h * sub, sub)
        y_copy(k, h).wait_recv()
        mine[k, where, :] = (
            part[k, pl.ds(pl.multiple_of(half * c + own_y + h * sub, 8), sub), :]
            + from_core[k, pl.ds(pl.multiple_of(own_y + h * sub, 8), sub), :]
            + from_y[k, where, :]
        )

    def hop(k, h, number):
        where = pl.ds(h * sub, sub)

        @pl.when(z == number)
        def _():
            if number == 0:
                fwd[k, where, :] = mine[k, where, :]
            else:
                fwd_copy(k, h).wait_recv()
                fwd[k, where, :] = mine[k, where, :] + from_left[k, where, :]
            fwd_copy(k, h).start()

        @pl.when(z == n_z - 1 - number)
        def _():
            if number == 0:
                bwd[k, where, :] = mine[k, where, :]
            else:
                bwd_copy(k, h).wait_recv()
                bwd[k, where, :] = mine[k, where, :] + from_right[k, where, :]
            bwd_copy(k, h).start()

    def finish(k, h):
        where = pl.ds(h * sub, sub)

        @pl.when(z == 0)
        def _():
            bwd_copy(k, h).wait_recv()
            total[k, where, :] = mine[k, where, :] + from_right[k, where, :]

        @pl.when(z == n_z - 1)
        def _():
            fwd_copy(k, h).wait_recv()
            total[k, where, :] = mine[k, where, :] + from_left[k, where, :]

        @pl.when(jnp.logical_and(z > 0, z < n_z - 1))
        def _():
            total[k, where, :] = mine[k, where, :] + (from_left[k, where, :] + from_right[k, where, :])

    def z_lanes(zz):
        return pl.ds(pl.multiple_of(zz * zrows, 128), zrows)

    def along_z(ref, k, d, sender):
        where = z_lanes((z - d + n_z) % n_z if sender else z)
        return remote(
            ref.at[:, where], ref.at[:, where], a_send.at[k, d - 1], a_recv.at[k, d - 1], z_peers[d - 1]
        )

    def out_copy(k, n):
        peer_plane = (2 * y + 1 - c, 2 * (1 - y) + c, 2 * (1 - y) + 1 - c)[n]
        rows_there = pl.ds(pl.multiple_of(peer_plane * rows, rows), rows)
        return remote(
            turned.at[k, rows_there, :], pieces.at[k, n], o_send.at[k, n], o_recv.at[k, n], plane_peers[n]
        )

    def turn(k, value):
        turned[k, :, pl.ds(0, quarter)] = value.T
        for n in range(3):
            out_copy(k, n).start()

    def assemble(k):
        for n in range(3):
            out_copy(k, n).wait_recv()
        own = turned[k, own_rows, :][:, :quarter]
        by_core, by_y, by_far = (pieces[k, n][:, :quarter] for n in range(3))
        low_y, low_core = y == 0, c == 0
        same = (jnp.where(low_y, own, by_y), jnp.where(low_y, by_y, own))
        other = (jnp.where(low_y, by_core, by_far), jnp.where(low_y, by_far, by_core))
        blocks = [jnp.where(low_core, same[n], other[n]) for n in range(2)]
        blocks += [jnp.where(low_core, other[n], same[n]) for n in range(2)]
        return jnp.concatenate(blocks, axis=1)

    def wait_along_z(ref, k):
        for d in range(1, n_z):
            along_z(ref, k, d, True).wait_recv()

    def chain(k):
        value = dot3(split(total[k]), split(g_inv[k]), NT)
        if k > 0:
            wait_along_z(solved.at[k - 1], k - 1)
            value = value - dot3(split(solved[k - 1]), split(g_chain[k - 1]), NT)
        solved[k, :, zlanes] = value
        for d in range(1, n_z):
            along_z(solved.at[k], k, d, False).start()
        turn(k, value)

    stage_a(0)
    weight_start(1, (0,))
    stage_a(1)
    stage_b(0)
    stage_a(2)
    stage_b(1)
    stage_a(3) if seps > 3 else None
    weight_start(0, (1, 2, 3, 4))
    for k in range(2, seps):
        stage_b(k)
    weight_start(1, (1, 2, 3, 4))
    for n in range(1):
        weight(0, n).wait_recv()
        weight(2, n).start()

    chunks = [(k, h) for k in range(seps) for h in range(HALVES)]
    for step in range(len(chunks) + LAG * (n_z - 1) + 1):
        if step < len(chunks):
            stage_c(*chunks[step])
        for number in range(n_z - 1):
            j = step - LAG * number
            if 0 <= j < len(chunks):
                hop(*chunks[j], number)
        j = step - LAG * (n_z - 2) - 1
        if 0 <= j < len(chunks):
            k, h = chunks[j]
            finish(k, h)
            if h == HALVES - 1:
                if k == 0:
                    for n in range(1, 5):
                        weight(0, n).wait_recv()
                        weight(2, n).start()
                    for way in (1, 2):
                        weight(way, 0).wait_recv()
                if k == 1:
                    for n in range(1, 5):
                        for way in (1, 2):
                            weight(way, n).wait_recv()
                chain(k)

    last = seps - 1
    root_rhs_t = g_rr[...].T
    turned_rr = part.at[0, :, pl.ds(0, zrows)]
    for k in range(seps):
        core_copy(k).wait_send()
    turned_rr[...] = root_rhs_t
    my_cols = pl.ds(pl.multiple_of(half * c + quarter * y, 8), quarter)
    wait_along_z(solved.at[last], last)
    term = dot3(split(solved[last]), split(g_rc[...]), NT)
    root_send[...] = term
    swap = remote(root_send, root_recv, x_send.at[0], x_recv.at[0], x_peer)
    swap.start()
    for k in range(seps):
        sep_out[k] = assemble(k)
    swap.wait_recv()
    root_full[:, zlanes] = part[0, my_cols, pl.ds(0, zrows)] - (term + root_recv[...])
    for d in range(1, n_z):
        along_z(root_full, seps, d, False).start()
    wait_along_z(root_full, seps)
    turn(seps, dot3(split(root_full[...]), split(g_ri[...]), NT))
    root_out[...] = assemble(seps)

    for way in range(3):
        for n in range(5):
            weight(way, n).wait_send()
    for k, h in chunks:
        y_copy(k, h).wait_send()

        @pl.when(z < n_z - 1)
        def _():
            fwd_copy(k, h).wait_send()

        @pl.when(z > 0)
        def _():
            bwd_copy(k, h).wait_send()

    for k in range(seps + 1):
        ref = solved.at[k] if k < seps else root_full
        for d in range(1, n_z):
            along_z(ref, k, d, False).wait_send()
        for n in range(3):
            out_copy(k, n).wait_send()
    swap.wait_send()


def fused(
    n_z,
    leaf_rhs,
    leaf_inverse,
    leaf_coupling,
    parent,
    sep_rhs,
    sep_inverse,
    sep_coupling,
    root_coupling,
    root_rhs,
    root_inverse,
):
    seps, rows, right = sep_rhs.shape[1:]
    width = sep_inverse.shape[3]
    zrows, half, quarter = width // n_z, right // 2, right // 4
    f32 = jnp.float32
    dma = pltpu.SemaphoreType.DMA
    vmem = pl.BlockSpec(memory_space=pltpu.VMEM)
    scratch = [
        (seps, zrows, width),
        (seps - 1, zrows, width),
        (zrows, width),
        (zrows, right),
        (zrows, width),
        (seps, right, width),
        (seps, half, width),
    ]
    scratch += [(seps, quarter, width)] * 9
    scratch += [
        (zrows, right),
        (seps + 1, zrows, 128),
        (seps + 1, 3, rows, 128),
        (quarter, zrows),
        (quarter, zrows),
        (quarter, width),
    ]
    sems = [(3, 5)] * 2 + [(seps,)] * 2 + [(seps, HALVES)] * 6
    sems += [(seps + 1, n_z - 1)] * 2 + [(seps + 1, 3)] * 2 + [(1,)] * 2
    sep, root = pl.pallas_call(
        functools.partial(kernel, n_z),
        out_shape=(
            jax.ShapeDtypeStruct((seps, rows, right), f32),
            jax.ShapeDtypeStruct((rows, right), f32),
        ),
        in_specs=[pl.BlockSpec(memory_space=pltpu.SMEM)] + [vmem] * 9,
        out_specs=(vmem, vmem),
        scratch_shapes=[pltpu.VMEM(s, f32) for s in scratch] + [dma(s) for s in sems],
        compiler_params=pltpu.CompilerParams(
            collective_id=0, has_side_effects=True, vmem_limit_bytes=60 * 2**20
        ),
        name="forward_solve",
    )(
        parent,
        leaf_rhs.reshape(leaf_rhs.shape[2:]),
        leaf_inverse.reshape(leaf_inverse.shape[2:]),
        leaf_coupling.reshape(leaf_coupling.shape[2:]),
        sep_rhs.reshape(sep_rhs.shape[1:]),
        sep_inverse.reshape(sep_inverse.shape[1:]),
        sep_coupling.reshape(sep_coupling.shape[1:]),
        root_coupling.reshape(root_coupling.shape[1:]),
        root_rhs,
        root_inverse,
    )
    return sep[None], root


def body(
    leaf_rhs,
    leaf_inverse,
    leaf_coupling,
    parent,
    sep_rhs,
    sep_inverse,
    sep_coupling,
    root_coupling,
    root_rhs,
    root_inverse,
):
    highest = lax.Precision.HIGHEST
    sep_count = sep_rhs.shape[1]
    row_count = sep_rhs.shape[2]
    row_start = lax.axis_index("row") * row_count
    leaf_solution = jnp.dot(leaf_inverse[0, 0], leaf_rhs[0, 0], precision=highest)
    levels = jnp.arange(sep_count, dtype=jnp.int32)
    keep_mask = (levels >= parent[0, 0]).astype(jnp.float32)

    def residual_term(k):
        coupled = jnp.dot(leaf_coupling[0, 0, k], leaf_solution, precision=highest) * keep_mask[k]
        own_rhs = lax.dynamic_update_slice_in_dim(
            jnp.zeros_like(coupled), sep_rhs[0, k], row_start, 0
        )
        return own_rhs - coupled

    residual_list = [lax.psum(residual_term(k), "row") for k in range(sep_count)]
    local_rows = [
        jnp.dot(sep_inverse[0, k], residual_list[k], precision=highest) for k in range(sep_count)
    ]
    solved = []
    gathered = None
    for k in range(sep_count):
        current = local_rows[k]
        if k > 0:
            current = current - jnp.dot(sep_coupling[0, k - 1], gathered, precision=highest)
        solved.append(current)
        gathered = lax.all_gather(current, "row", axis=0, tiled=True)
    sep_out = jnp.stack(solved)[None]
    root_term = jnp.dot(root_coupling[0], gathered, precision=highest)
    root_sum = lax.psum(root_term, "layer")
    root_residual = root_rhs - root_sum
    root_out = jnp.dot(
        root_inverse, lax.all_gather(root_residual, "row", axis=0, tiled=True), precision=highest
    )
    return (sep_out, root_out)


def solution(mesh):
    n_layer, n_row = mesh.shape["layer"], mesh.shape["row"]

    def per_device(*arrays):
        right, width = arrays[0].shape[3], arrays[5].shape[3]
        n_z = n_row // 4
        fits = (
            n_layer == 2
            and n_row in (8, 16)
            and width % (128 * n_z) == 0
            and right % (32 * HALVES) == 0
            and right // 4 <= 128
            and arrays[4].shape[1] >= 3
        )
        return functools.partial(fused, n_z)(*arrays) if fits else body(*arrays)

    return jax.shard_map(
        per_device,
        mesh=mesh,
        in_specs=(
            P("layer", "row", None, None),
            P("layer", "row", None, None),
            P("layer", "row", None, None, None),
            P("layer", "row"),
            P("layer", None, "row", None),
            P("layer", None, "row", None),
            P("layer", None, "row", None),
            P("layer", "row", None),
            P("row", None),
            P("row", None),
        ),
        out_specs=(P("layer", None, "row", None), P("row", None)),
        check_vma=False,
    )
```

```python
import functools

import jax
import jax.numpy as jnp
from jax import lax
from jax.experimental import pallas as pl
from jax.experimental.pallas import tpu as pltpu
from jax.sharding import PartitionSpec as P

MESH = pl.DeviceIdType.MESH
NN = (((1,), (0,)), ((), ()))
NT = (((1,), (1,)), ((), ()))
HALVES = 2
LAG = 2


def split(a):
    high = a.astype(jnp.bfloat16)
    return high, (a - high.astype(jnp.float32)).astype(jnp.bfloat16)


def dot3(a, b, dims):
    (ah, al), (bh, bl) = a, b
    dot = functools.partial(lax.dot_general, dimension_numbers=dims, preferred_element_type=jnp.float32)
    return dot(ah, bh) + (dot(ah, bl) + dot(al, bh))


def kernel(
    n_z,
    parent,
    leaf_rhs,
    leaf_inverse,
    leaf_coupling,
    sep_rhs,
    sep_inverse,
    sep_coupling,
    root_coupling,
    root_rhs,
    root_inverse,
    sep_out,
    root_out,
    g_inv,
    g_chain,
    g_rc,
    g_rr,
    g_ri,
    part,
    from_core,
    to_y,
    from_y,
    mine,
    fwd,
    bwd,
    from_left,
    from_right,
    total,
    solved,
    padded,
    turned,
    pieces,
    root_send,
    root_recv,
    root_full,
    w_send,
    w_recv,
    c_send,
    c_recv,
    y_send,
    y_recv,
    f_send,
    f_recv,
    b_send,
    b_recv,
    a_send,
    a_recv,
    o_send,
    o_recv,
    x_send,
    x_recv,
):
    seps, rows, right = sep_rhs.shape
    width = sep_inverse.shape[2]
    zrows = width // n_z
    half, quarter = right // 2, right // 4
    sub = quarter // HALVES

    layer = lax.axis_index("layer")
    me = lax.axis_index("row")
    z, y, c = me // 4, (me // 2) % 2, me % 2
    plane = 2 * y + c
    base = 4 * z

    def at(zz, yy, cc):
        return (layer, 4 * zz + 2 * yy + cc)

    core_peer = at(z, y, 1 - c)
    y_peer = at(z, 1 - y, c)
    far_peer = at(z, 1 - y, 1 - c)
    x_peer = (1 - layer, me)
    left, right_peer = (layer, me - 4), (layer, me + 4)
    z_peers = [at((z + d) % n_z, y, c) for d in range(1, n_z)]
    plane_peers = [core_peer, y_peer, far_peer]

    def remote(src, dst, send, recv, peer):
        return pltpu.make_async_remote_copy(
            src_ref=src, dst_ref=dst, send_sem=send, recv_sem=recv, device_id=peer, device_id_type=MESH
        )

    barrier = pltpu.get_barrier_semaphore()
    peers = plane_peers + z_peers + [x_peer]
    for peer in peers:
        pl.semaphore_signal(barrier, inc=1, device_id=peer, device_id_type=MESH)
    pl.semaphore_wait(barrier, len(peers))

    own_rows = pl.ds(pl.multiple_of(plane * rows, rows), rows)
    y_rows = pl.ds(pl.multiple_of((2 * (1 - y) + c) * rows, rows), rows)
    weights = [
        (sep_inverse, g_inv, True),
        (sep_coupling, g_chain, True),
        (root_coupling, g_rc, False),
        (root_rhs, g_rr, False),
        (root_inverse, g_ri, False),
    ]

    def slot(ref, deep, where):
        return ref.at[:, where, :] if deep else ref.at[where, :]

    def weight(way, n):
        source, dest, deep = weights[n]
        if way == 2:
            source, where = slot(dest, deep, y_rows), y_rows
        else:
            where = own_rows
        return remote(
            source,
            slot(dest, deep, where),
            w_send.at[way, n],
            w_recv.at[way, n],
            y_peer if way == 0 else core_peer,
        )

    def weight_start(way, which):
        for n in which:
            weight(way, n).start()

    weight_start(0, (0,))
    g_inv[:, own_rows, :] = sep_inverse[...]
    g_chain[:, own_rows, :] = sep_coupling[...]
    g_rc[own_rows, :] = root_coupling[...]
    g_rr[own_rows, :] = root_rhs[...]
    g_ri[own_rows, :] = root_inverse[...]

    leaf = dot3(split(leaf_inverse[...]), split(leaf_rhs[...]), NN)
    leaf_t = split(leaf.T)
    zlanes = pl.ds(pl.multiple_of(z * zrows, 128), zrows)
    core_cols = pl.ds(pl.multiple_of(half * c, 8), half)
    other_core_cols = pl.ds(pl.multiple_of(half * (1 - c), 8), half)
    padded[...] = jnp.zeros_like(padded)

    def core_copy(k):
        return remote(
            part.at[k, other_core_cols, :], from_core.at[k], c_send.at[k], c_recv.at[k], core_peer
        )

    def stage_a(k):
        keep = jnp.where(parent[0, 0] <= k, -1.0, 0.0).astype(jnp.float32)
        part[k] = dot3(leaf_t, split(leaf_coupling[k]), NT) * keep
        padded[own_rows, :] = sep_rhs[k]
        part[k, :, zlanes] += padded[...].T
        core_copy(k).start()

    own_y = pl.multiple_of(quarter * y, 8)
    peer_y = pl.multiple_of(quarter * (1 - y), 8)

    def y_copy(k, h):
        where = pl.ds(h * sub, sub)
        return remote(
            to_y.at[k, where, :], from_y.at[k, where, :], y_send.at[k, h], y_recv.at[k, h], y_peer
        )

    def stage_b(k):
        core_copy(k).wait_recv()
        to_y[k] = (
            part[k, pl.ds(pl.multiple_of(half * c + peer_y, 8), quarter), :]
            + from_core[k, pl.ds(peer_y, quarter), :]
        )
        for h in range(HALVES):
            y_copy(k, h).start()

    def fwd_copy(k, h):
        where = pl.ds(h * sub, sub)
        return remote(
            fwd.at[k, where, :], from_left.at[k, where, :], f_send.at[k, h], f_recv.at[k, h], right_peer
        )

    def bwd_copy(k, h):
        where = pl.ds(h * sub, sub)
        return remote(
            bwd.at[k, where, :], from_right.at[k, where, :], b_send.at[k, h], b_recv.at[k, h], left
        )

    def stage_c(k, h):
        where = pl.ds(h * sub, sub)
        y_copy(k, h).wait_recv()
        mine[k, where, :] = (
            part[k, pl.ds(pl.multiple_of(half * c + own_y + h * sub, 8), sub), :]
            + from_core[k, pl.ds(pl.multiple_of(own_y + h * sub, 8), sub), :]
            + from_y[k, where, :]
        )

    def hop(k, h, number):
        where = pl.ds(h * sub, sub)

        @pl.when(z == number)
        def _():
            if number == 0:
                fwd[k, where, :] = mine[k, where, :]
            else:
                fwd_copy(k, h).wait_recv()
                fwd[k, where, :] = mine[k, where, :] + from_left[k, where, :]
            fwd_copy(k, h).start()

        @pl.when(z == n_z - 1 - number)
        def _():
            if number == 0:
                bwd[k, where, :] = mine[k, where, :]
            else:
                bwd_copy(k, h).wait_recv()
                bwd[k, where, :] = mine[k, where, :] + from_right[k, where, :]
            bwd_copy(k, h).start()

    def finish(k, h):
        where = pl.ds(h * sub, sub)

        @pl.when(z == 0)
        def _():
            bwd_copy(k, h).wait_recv()
            total[k, where, :] = mine[k, where, :] + from_right[k, where, :]

        @pl.when(z == n_z - 1)
        def _():
            fwd_copy(k, h).wait_recv()
            total[k, where, :] = mine[k, where, :] + from_left[k, where, :]

        @pl.when(jnp.logical_and(z > 0, z < n_z - 1))
        def _():
            total[k, where, :] = mine[k, where, :] + (from_left[k, where, :] + from_right[k, where, :])

    def z_lanes(zz):
        return pl.ds(pl.multiple_of(zz * zrows, 128), zrows)

    def along_z(ref, k, d, sender):
        where = z_lanes((z - d + n_z) % n_z if sender else z)
        return remote(
            ref.at[:, where], ref.at[:, where], a_send.at[k, d - 1], a_recv.at[k, d - 1], z_peers[d - 1]
        )

    def out_copy(k, n):
        peer_plane = (2 * y + 1 - c, 2 * (1 - y) + c, 2 * (1 - y) + 1 - c)[n]
        rows_there = pl.ds(pl.multiple_of(peer_plane * rows, rows), rows)
        return remote(
            turned.at[k, rows_there, :], pieces.at[k, n], o_send.at[k, n], o_recv.at[k, n], plane_peers[n]
        )

    def turn(k, value):
        turned[k, :, pl.ds(0, quarter)] = value.T
        for n in range(3):
            out_copy(k, n).start()

    def assemble(k):
        for n in range(3):
            out_copy(k, n).wait_recv()
        own = turned[k, own_rows, :][:, :quarter]
        by_core, by_y, by_far = (pieces[k, n][:, :quarter] for n in range(3))
        low_y, low_core = y == 0, c == 0
        same = (jnp.where(low_y, own, by_y), jnp.where(low_y, by_y, own))
        other = (jnp.where(low_y, by_core, by_far), jnp.where(low_y, by_far, by_core))
        blocks = [jnp.where(low_core, same[n], other[n]) for n in range(2)]
        blocks += [jnp.where(low_core, other[n], same[n]) for n in range(2)]
        return jnp.concatenate(blocks, axis=1)

    def wait_along_z(ref, k):
        for d in range(1, n_z):
            along_z(ref, k, d, True).wait_recv()

    def chain(k):
        value = dot3(split(total[k]), split(g_inv[k]), NT)
        if k > 0:
            wait_along_z(solved.at[k - 1], k - 1)
            value = value - dot3(split(solved[k - 1]), split(g_chain[k - 1]), NT)
        solved[k, :, zlanes] = value
        for d in range(1, n_z):
            along_z(solved.at[k], k, d, False).start()
        turn(k, value)

    stage_a(0)
    weight_start(1, (0,))
    stage_a(1)
    stage_b(0)
    chunks = [(k, h) for k in range(seps) for h in range(HALVES)]

    def ahead(step):
        k = step // HALVES + 2
        if step % HALVES == 0 and k < seps:
            stage_a(k)
            stage_b(k - 1)
        if step == HALVES * (seps - 2):
            stage_b(seps - 1)
            weight_start(1, (1, 2, 3, 4))
            weight_start(0, (1, 2, 3, 4))
            for n in (0,):
                weight(0, n).wait_recv()
                weight(2, n).start()

    for step in range(len(chunks) + LAG * (n_z - 1) + 1):
        ahead(step)
        for number in reversed(range(n_z - 1)):
            j = step - LAG * number
            if 0 <= j < len(chunks):
                if number == 0:
                    stage_c(*chunks[j])
                hop(*chunks[j], number)
        j = step - LAG * (n_z - 1)
        if 0 <= j < len(chunks):
            k, h = chunks[j]
            finish(k, h)
            if h == HALVES - 1:
                if k == 0:
                    weight(0, 1).wait_recv()
                    weight(2, 1).start()
                if k < 2:
                    for way in (1, 2):
                        weight(way, k).wait_recv()
                if k == seps - 1:
                    for n in range(2, 5):
                        weight(0, n).wait_recv()
                        weight(2, n).start()
                chain(k)

    last = seps - 1
    for n in range(2, 5):
        for way in (1, 2):
            weight(way, n).wait_recv()
    root_rhs_t = g_rr[...].T
    turned_rr = part.at[0, :, pl.ds(0, zrows)]
    for k in range(seps):
        core_copy(k).wait_send()
    turned_rr[...] = root_rhs_t
    my_cols = pl.ds(pl.multiple_of(half * c + quarter * y, 8), quarter)
    wait_along_z(solved.at[last], last)
    term = dot3(split(solved[last]), split(g_rc[...]), NT)
    root_send[...] = term
    swap = remote(root_send, root_recv, x_send.at[0], x_recv.at[0], x_peer)
    swap.start()
    for k in range(seps):
        sep_out[k] = assemble(k)
    swap.wait_recv()
    root_full[:, zlanes] = part[0, my_cols, pl.ds(0, zrows)] - (term + root_recv[...])
    for d in range(1, n_z):
        along_z(root_full, seps, d, False).start()
    wait_along_z(root_full, seps)
    turn(seps, dot3(split(root_full[...]), split(g_ri[...]), NT))
    root_out[...] = assemble(seps)

    for way in range(3):
        for n in range(5):
            weight(way, n).wait_send()
    for k, h in chunks:
        y_copy(k, h).wait_send()

        @pl.when(z < n_z - 1)
        def _():
            fwd_copy(k, h).wait_send()

        @pl.when(z > 0)
        def _():
            bwd_copy(k, h).wait_send()

    for k in range(seps + 1):
        ref = solved.at[k] if k < seps else root_full
        for d in range(1, n_z):
            along_z(ref, k, d, False).wait_send()
        for n in range(3):
            out_copy(k, n).wait_send()
    swap.wait_send()


def fused(
    n_z,
    leaf_rhs,
    leaf_inverse,
    leaf_coupling,
    parent,
    sep_rhs,
    sep_inverse,
    sep_coupling,
    root_coupling,
    root_rhs,
    root_inverse,
):
    seps, rows, right = sep_rhs.shape[1:]
    width = sep_inverse.shape[3]
    zrows, half, quarter = width // n_z, right // 2, right // 4
    f32 = jnp.float32
    dma = pltpu.SemaphoreType.DMA
    vmem = pl.BlockSpec(memory_space=pltpu.VMEM)
    scratch = [
        (seps, zrows, width),
        (seps - 1, zrows, width),
        (zrows, width),
        (zrows, right),
        (zrows, width),
        (seps, right, width),
        (seps, half, width),
    ]
    scratch += [(seps, quarter, width)] * 9
    scratch += [
        (zrows, right),
        (seps + 1, zrows, 128),
        (seps + 1, 3, rows, 128),
        (quarter, zrows),
        (quarter, zrows),
        (quarter, width),
    ]
    sems = [(3, 5)] * 2 + [(seps,)] * 2 + [(seps, HALVES)] * 6
    sems += [(seps + 1, n_z - 1)] * 2 + [(seps + 1, 3)] * 2 + [(1,)] * 2
    sep, root = pl.pallas_call(
        functools.partial(kernel, n_z),
        out_shape=(
            jax.ShapeDtypeStruct((seps, rows, right), f32),
            jax.ShapeDtypeStruct((rows, right), f32),
        ),
        in_specs=[pl.BlockSpec(memory_space=pltpu.SMEM)] + [vmem] * 9,
        out_specs=(vmem, vmem),
        scratch_shapes=[pltpu.VMEM(s, f32) for s in scratch] + [dma(s) for s in sems],
        compiler_params=pltpu.CompilerParams(
            collective_id=0, has_side_effects=True, vmem_limit_bytes=60 * 2**20
        ),
        name="forward_solve",
    )(
        parent,
        leaf_rhs.reshape(leaf_rhs.shape[2:]),
        leaf_inverse.reshape(leaf_inverse.shape[2:]),
        leaf_coupling.reshape(leaf_coupling.shape[2:]),
        sep_rhs.reshape(sep_rhs.shape[1:]),
        sep_inverse.reshape(sep_inverse.shape[1:]),
        sep_coupling.reshape(sep_coupling.shape[1:]),
        root_coupling.reshape(root_coupling.shape[1:]),
        root_rhs,
        root_inverse,
    )
    return sep[None], root


def body(
    leaf_rhs,
    leaf_inverse,
    leaf_coupling,
    parent,
    sep_rhs,
    sep_inverse,
    sep_coupling,
    root_coupling,
    root_rhs,
    root_inverse,
):
    highest = lax.Precision.HIGHEST
    sep_count = sep_rhs.shape[1]
    row_count = sep_rhs.shape[2]
    row_start = lax.axis_index("row") * row_count
    leaf_solution = jnp.dot(leaf_inverse[0, 0], leaf_rhs[0, 0], precision=highest)
    levels = jnp.arange(sep_count, dtype=jnp.int32)
    keep_mask = (levels >= parent[0, 0]).astype(jnp.float32)

    def residual_term(k):
        coupled = jnp.dot(leaf_coupling[0, 0, k], leaf_solution, precision=highest) * keep_mask[k]
        own_rhs = lax.dynamic_update_slice_in_dim(
            jnp.zeros_like(coupled), sep_rhs[0, k], row_start, 0
        )
        return own_rhs - coupled

    residual_list = [lax.psum(residual_term(k), "row") for k in range(sep_count)]
    local_rows = [
        jnp.dot(sep_inverse[0, k], residual_list[k], precision=highest) for k in range(sep_count)
    ]
    solved = []
    gathered = None
    for k in range(sep_count):
        current = local_rows[k]
        if k > 0:
            current = current - jnp.dot(sep_coupling[0, k - 1], gathered, precision=highest)
        solved.append(current)
        gathered = lax.all_gather(current, "row", axis=0, tiled=True)
    sep_out = jnp.stack(solved)[None]
    root_term = jnp.dot(root_coupling[0], gathered, precision=highest)
    root_sum = lax.psum(root_term, "layer")
    root_residual = root_rhs - root_sum
    root_out = jnp.dot(
        root_inverse, lax.all_gather(root_residual, "row", axis=0, tiled=True), precision=highest
    )
    return (sep_out, root_out)


def solution(mesh):
    n_layer, n_row = mesh.shape["layer"], mesh.shape["row"]

    def per_device(*arrays):
        right, width = arrays[0].shape[3], arrays[5].shape[3]
        n_z = n_row // 4
        fits = (
            n_layer == 2
            and n_row in (8, 16)
            and width % (128 * n_z) == 0
            and right % (32 * HALVES) == 0
            and right // 4 <= 128
            and arrays[4].shape[1] >= 3
        )
        return functools.partial(fused, n_z)(*arrays) if fits else body(*arrays)

    return jax.shard_map(
        per_device,
        mesh=mesh,
        in_specs=(
            P("layer", "row", None, None),
            P("layer", "row", None, None),
            P("layer", "row", None, None, None),
            P("layer", "row"),
            P("layer", None, "row", None),
            P("layer", None, "row", None),
            P("layer", None, "row", None),
            P("layer", "row", None),
            P("row", None),
            P("row", None),
        ),
        out_specs=(P("layer", None, "row", None), P("row", None)),
        check_vma=False,
    )
```
